128 devices in a mesh: corpus: 16 (over z, y), fsdp: 2 (over core), tensor: 4 (over x).
Axes of the slice: x: 4, y: 4, z: 4, core: 2. Of those that a mesh axis runs over, the one named last changes fastest.
Arguments:
- queries_in: bfloat16 [4096, 4096], P(('corpus', 'fsdp')), may hold values from -6 to 6
- head_weight: bfloat16 [4096, 4096], P('fsdp', 'tensor'), may hold values from -0.09375 to 0.09375
- passages: bfloat16 [16384, 4096], P('corpus', 'tensor'), may hold values from -0.15625 to 0.15625
- teacher: float32 [4096, 4, 32], P(('corpus', 'fsdp')), may hold values from -250 to 400
- cand_block: int32 [4096, 4], P(('corpus', 'fsdp')), may hold values from 0 to 127, all different within a row; in each aligned block of 128 rows (0 to 127, 128 to 255, ...) at most 6 rows name the same one
- cand_offset: int32 [4096, 4, 32], P(('corpus', 'fsdp')), may hold values from 0 to 127, as said below
- block_slot: int32 [128], replicated, may hold values from 0 to 127, each once
Outputs:
- kl_loss: float32 [4096], P(('corpus', 'fsdp'))
- head_grad: float32 [4096, 4096], P('fsdp', 'tensor')
The draws below stay inside these ranges and needn't reach their ends.
Inputs may be any that keep to these rules, and one draw needn't show every extreme that they name: `cand_block`: in the rows of one device no block id appears more than 6 times, and some block id appears exactly 6 times there; the 4 ids of one query differ. `cand_offset`: the 32 offsets of one query in one block differ. `block_slot`: each storage position is taken by exactly one block.
All inputs are finite; a program needn't handle non-finite values.
Results may differ from the reference program's by a relative error of at most 0.012.
The reference program's roundings to bfloat16 on the way (of `query`, `dscore`, `block_part` and `query_grad`) count: a program that leaves them out, or rounds other values in their place, can miss the bound.
Values may be sent and summed in bfloat16 or wider, within the bound.
A program may use at most 128 MiB of HBM per device.

```python
import math
import jax
import jax.numpy as jnp
import numpy as np
from jax import lax

D = 4096
QDEV = 128
G = 4
OFFS = 32
ROWS = 128
NB = 128
MOSTB = 6
Q = 4096


def draw_passages(key, part):
    sigma = 0.04 / D ** 0.5
    first, second = jax.random.split(key, 2)
    base = jax.random.truncated_normal(first, -4.0, 4.0, (NB * ROWS, D), jnp.float32)
    spread = jnp.exp(jax.random.uniform(second, (NB * ROWS, 1), jnp.float32, -0.7, 0.7))
    return (sigma * spread * base).astype(jnp.bfloat16)


def draw_teacher(key, part):
    first, second = jax.random.split(key, 2)
    base = jax.random.truncated_normal(first, -4.0, 4.0, (Q, G, OFFS), jnp.float32)
    spread = jnp.exp(jax.random.uniform(second, (Q, 1, 1), jnp.float32, -0.7, 0.7))
    return 2.0 * spread * base


def draw_cand_offset(key, part):
    raw_keys = jax.random.randint(key, (Q, G, ROWS), 0, 1 << 20, jnp.int32)
    keyed = raw_keys * ROWS + lax.broadcasted_iota(jnp.int32, (Q, G, ROWS), 2)
    ordering = jnp.argsort(keyed, axis=2, stable=True)
    return ordering[:, :, :OFFS].astype(jnp.int32)


def levels(rng, shape, cuts, low, high):
    def one(axis_at, blocks):
        draws = jax.random.uniform(jax.random.fold_in(jax.random.fold_in(rng, 6), axis_at), (blocks,), jnp.float32, low / len(cuts), high / len(cuts))
        return jnp.repeat(jnp.exp(draws), shape[axis_at] // blocks).reshape((-1,) + (1,) * (len(shape) - axis_at - 1))

    level = one(*cuts[0])
    for cut in cuts[1:]:
        level = level * one(*cut)
    return level


def deal_out(key, own, number, rows, number_of, top, limit, skew):
    sequence = jax.random.permutation(key, number_of)
    crowded, ordinary = load_shares(number_of, rows * top, limit, skew, True), load_shares(number_of, rows * top, limit, skew, False)
    places = jnp.arange(number_of)

    def named(tallies, turn):
        used = int((tallies > 0).sum())
        fixed = max(1, used // 4)
        moved = fixed + (places - fixed + turn * (used - fixed)) % max(1, number_of - fixed)
        return jnp.zeros((number_of,), jnp.int32).at[sequence[jnp.where(places < fixed, places, moved)]].set(jnp.asarray(tallies, jnp.int32))

    tallies = jnp.where(number % 4 == 0, named(crowded, number // 4), named(ordinary, number - number // 4 - 1))
    mixed = jax.random.permutation(jax.random.fold_in(own, 3), number_of)
    giver, receiver = mixed[0:number_of // 2 * 2:2], mixed[1:number_of // 2 * 2:2]
    room = jnp.minimum(tallies[giver] - 1, limit - tallies[receiver]) // 2
    room = jnp.where((giver == sequence[0]) | (receiver == sequence[0]) | (tallies[receiver] == 0), 0, jnp.maximum(room, 0))
    moved = jax.random.randint(jax.random.fold_in(own, 4), (number_of // 2,), 0, 1 << 20) % (room + 1)
    tallies = tallies.at[giver].add(-moved).at[receiver].add(moved)
    labels = jnp.searchsorted(jnp.cumsum(tallies), jnp.arange(rows * top), side="right").astype(jnp.int32)
    grid = labels.reshape(top, rows).T
    grid = grid[jax.random.permutation(jax.random.fold_in(own, 1), rows)]
    turn = jax.random.randint(jax.random.fold_in(own, 2), (rows, 1), 0, top)
    return jnp.take_along_axis(grid, (jnp.arange(top)[None, :] + turn) % top, axis=1)


def load_shares(count, total, reach, slope, full):
    portions = [(1 << 20) // math.isqrt(grade ** slope) + 1 for grade in range(1, count + 1)]
    largest = reach if full else min(reach, max(-(-total // count), total * portions[0] // sum(portions)))
    least = 1 if total - largest >= count - 1 else 0
    holding, rest = [largest] + [least] * (count - 1), total - largest - least * (count - 1)
    while rest > 0:
        free = [i for i in range(1, count) if holding[i] < largest] or [i for i in range(1, count) if holding[i] < reach]
        mass, budget = sum([portions[i] for i in free]), rest
        for i in free:
            more = min(reach - holding[i], max(1, budget * portions[i] // mass), rest)
            holding[i] = holding[i] + more
            rest = rest - more
    return np.array(holding)


def gaussian(stream_key, shape, deviation, reach, cuts=(), kind=jnp.bfloat16):
    result = deviation * jax.random.normal(stream_key, shape, jnp.float32)
    if cuts:
        result = result * levels(stream_key, shape, cuts, -0.22, 0.18)
    return jnp.clip(result, -reach, reach).astype(kind)


def setup_inputs(seed: int = 0) -> dict:
    seeds = jax.random.split(jax.random.key(seed), 8)
    queries_in = gaussian(seeds[0], (Q, D), 1.0, 6.0, ((0, 32),))
    head_weight = gaussian(seeds[1], (D, D), D ** -0.5, 0.09375, ((0, 2), (1, 4)))
    passages = draw_passages(jax.random.fold_in(seeds[7], 71), 0)
    teacher = draw_teacher(jax.random.fold_in(seeds[7], 71), 0)
    cand_block_keys = jax.random.split(jax.random.fold_in(seeds[4], 1), Q // QDEV)
    cand_block_turns = jax.random.permutation(jax.random.fold_in(seeds[4], 3), Q // QDEV)
    cand_block = jax.vmap(lambda own, number: deal_out(jax.random.fold_in(seeds[4], 2), own, number, QDEV, NB, G, MOSTB, 2))(cand_block_keys, cand_block_turns).reshape((Q, G))
    cand_offset = draw_cand_offset(jax.random.fold_in(seeds[7], 71), 0)
    block_slot = jax.random.permutation(seeds[6], NB).astype(jnp.int32)
    return dict(queries_in=queries_in, head_weight=head_weight, passages=passages, teacher=teacher, cand_block=cand_block, cand_offset=cand_offset, block_slot=block_slot)


def reference(queries_in, head_weight, passages, teacher, cand_block, cand_offset, block_slot):
    query = jnp.dot(queries_in, head_weight, preferred_element_type=jnp.float32).astype(jnp.bfloat16)
    cand_rows = (block_slot[cand_block] * ROWS).astype(jnp.int32)[:, :, None] + cand_offset.astype(jnp.int32)
    block_count = query.shape[0] // 16

    def per_block(inputs_block):
        query_block, rows_block, teacher_block = inputs_block
        embedded = passages[rows_block].astype(jnp.float32)
        student = 50.0 * jnp.einsum("id,igkd->igk", query_block.astype(jnp.float32), embedded)
        log_student = student - jax.nn.logsumexp(student, axis=(1, 2), keepdims=True)
        log_teacher = teacher_block - jax.nn.logsumexp(teacher_block, axis=(1, 2), keepdims=True)
        prob_teacher = jnp.exp(log_teacher)
        kl_part = jnp.sum(prob_teacher * (log_teacher - log_student), axis=(1, 2))
        dscore = (50.0 * (jnp.exp(log_student) - prob_teacher)).astype(jnp.bfloat16)
        block_part = jnp.einsum("igk,igkd->igd", dscore.astype(jnp.float32), embedded).astype(jnp.bfloat16)
        query_grad = jnp.sum(block_part.astype(jnp.float32), axis=1).astype(jnp.bfloat16)
        return kl_part, query_grad

    kl_loss, query_grad = lax.map(
        per_block,
        (query.reshape(block_count, 16, D), cand_rows.reshape(block_count, 16, G, OFFS),
         teacher.reshape(block_count, 16, G, OFFS)))
    query_grad = query_grad.reshape(-1, D)
    head_grad = lax.dot_general(queries_in, query_grad, (((0,), (0,)), ((), ())),
                                preferred_element_type=jnp.float32)
    return kl_loss.reshape(-1), head_grad
```

```python
import jax
import jax.numpy as jnp
from jax import lax
from jax.sharding import PartitionSpec as P

ROWS = 128
MOSTB = 6
SWAP = [(0, 1), (1, 0)]


def on_device(queries_in, head_weight, passages, teacher, cand_block, cand_offset, block_slot):
    query_rows, width = queries_in.shape
    half = width // 2
    cols = head_weight.shape[1]
    per_query = cand_block.shape[1]
    offset_count = cand_offset.shape[2]
    total_blocks = block_slot.shape[0]
    n_corpus = lax.axis_size("corpus")
    blocks_here = passages.shape[0] // ROWS
    slot_total = total_blocks * MOSTB
    slots_each = blocks_here * MOSTB
    picks = query_rows * per_query
    first = lax.axis_index("fsdp") == 0

    low, high = queries_in[:, :half], queries_in[:, half:]
    mine = jnp.where(first, low, high)
    other = jnp.where(first, high, low)
    theirs = lax.ppermute(other, "fsdp", SWAP)
    part_theirs = jnp.dot(theirs, head_weight, preferred_element_type=jnp.float32)
    back = lax.ppermute(part_theirs, "fsdp", SWAP)
    part_mine = jnp.dot(mine, head_weight, preferred_element_type=jnp.float32)
    query = (part_mine + back).astype(jnp.bfloat16)
    all_mine = lax.all_gather(mine, "corpus", axis=0, tiled=True)
    all_theirs = lax.all_gather(theirs, "corpus", axis=0, tiled=True)

    block_ids = lax.broadcasted_iota(jnp.int32, (1, total_blocks), 1)
    named = (cand_block.reshape(-1, 1) == block_ids).astype(jnp.int32)
    slot_of = jnp.sum(named * block_slot.reshape(1, -1), axis=1)
    hits = slot_of[:, None] == block_ids
    before = (
        lax.broadcasted_iota(jnp.int32, (picks, picks), 1)
        < lax.broadcasted_iota(jnp.int32, (picks, picks), 0)
    ).astype(jnp.bfloat16)
    earlier = jnp.dot(before, hits.astype(jnp.bfloat16), preferred_element_type=jnp.float32)
    slot_rank = jnp.sum(jnp.where(hits, earlier, 0.0), axis=1).astype(jnp.int32)
    position = slot_of * MOSTB + slot_rank

    slot_ids = lax.broadcasted_iota(jnp.int32, (slot_total, 1), 0)
    place = (slot_ids == position.reshape(1, -1)).astype(jnp.bfloat16)
    by_query = position.reshape(query_rows, per_query)
    owner = slot_ids == by_query[:, 0].reshape(1, -1)
    for g in range(1, per_query):
        owner = owner | (slot_ids == by_query[:, g].reshape(1, -1))
    owner = owner.astype(jnp.bfloat16)
    slot_block = (slot_ids % slots_each) // MOSTB

    send_queries = jnp.dot(owner, query, preferred_element_type=jnp.float32).astype(jnp.bfloat16)
    got_queries = lax.all_to_all(
        send_queries.reshape(n_corpus, slots_each, cols), "corpus", 0, 0, tiled=True
    ).reshape(slot_total, cols)
    wide = lax.dot_general(
        got_queries, passages, (((1,), (1,)), ((), ())), preferred_element_type=jnp.float32
    )
    scores = wide[:, :ROWS]
    for j in range(1, blocks_here):
        scores = jnp.where(slot_block == j, wide[:, j * ROWS : (j + 1) * ROWS], scores)
    returned = lax.all_to_all(
        scores.reshape(n_corpus, slots_each, ROWS), "corpus", 0, 0, tiled=True
    ).reshape(slot_total, ROWS)

    picked = returned[position]
    offsets = cand_offset.reshape(picks, offset_count)
    row_ids = lax.broadcasted_iota(jnp.int32, (1, 1, ROWS), 2)
    chosen = offsets[:, :, None] == row_ids
    partial = jnp.sum(jnp.where(chosen, picked[:, None, :], 0.0), axis=2)
    total = partial.reshape(query_rows, per_query * offset_count)
    total = total + lax.ppermute(total, "tensor", [(0, 1), (1, 0), (2, 3), (3, 2)])
    total = total + lax.ppermute(total, "tensor", [(0, 2), (2, 0), (1, 3), (3, 1)])
    student = 50.0 * total

    cached = teacher.reshape(query_rows, per_query * offset_count)
    log_student = student - jax.nn.logsumexp(student, axis=1, keepdims=True)
    log_teacher = cached - jax.nn.logsumexp(cached, axis=1, keepdims=True)
    prob_teacher = jnp.exp(log_teacher)
    kl_loss = jnp.sum(prob_teacher * (log_teacher - log_student), axis=1)
    dscore = (50.0 * (jnp.exp(log_student) - prob_teacher)).astype(jnp.bfloat16)

    spread = jnp.sum(
        jnp.where(chosen, dscore.reshape(picks, offset_count, 1).astype(jnp.float32), 0.0), axis=1
    ).astype(jnp.bfloat16)
    dense = jnp.dot(place, spread, preferred_element_type=jnp.float32).astype(jnp.bfloat16)
    got_dense = lax.all_to_all(
        dense.reshape(n_corpus, slots_each, ROWS), "corpus", 0, 0, tiled=True
    ).reshape(slot_total, ROWS)
    expanded = jnp.concatenate(
        [jnp.where(slot_block == j, got_dense, jnp.bfloat16(0)) for j in range(blocks_here)], axis=1
    )
    block_part = jnp.dot(expanded, passages, preferred_element_type=jnp.float32).astype(jnp.bfloat16)
    arrived = lax.all_to_all(
        block_part.reshape(n_corpus, slots_each, cols), "corpus", 0, 0, tiled=True
    ).reshape(slot_total, cols)
    query_grad = lax.dot_general(
        owner, arrived, (((0,), (0,)), ((), ())), preferred_element_type=jnp.float32
    ).astype(jnp.bfloat16)

    grad_mine = lax.all_gather(query_grad, "corpus", axis=0, tiled=True)
    grad_theirs = lax.ppermute(grad_mine, "fsdp", SWAP)
    across = (((0,), (0,)), ((), ()))
    head_grad = lax.dot_general(
        all_mine, grad_mine, across, preferred_element_type=jnp.float32
    ) + lax.dot_general(all_theirs, grad_theirs, across, preferred_element_type=jnp.float32)
    return (kl_loss, head_grad)


def solution(mesh):
    placed = (
        P(("corpus", "fsdp"), None),
        P("fsdp", "tensor"),
        P("corpus", "tensor"),
        P(("corpus", "fsdp"), None, None),
        P(("corpus", "fsdp"), None),
        P(("corpus", "fsdp"), None, None),
        P(),
    )
    return jax.shard_map(
        on_device,
        mesh=mesh,
        in_specs=placed,
        out_specs=(P(("corpus", "fsdp")), P("fsdp", "tensor")),
        check_vma=False,
    )
```
